256 devices in a mesh: hi: 16 (over x, y), lo: 16 (over z, core).
Axes of the slice: x: 4, y: 4, z: 8, core: 2. Of those that a mesh axis runs over, the one named last changes fastest.
Arguments:
- queries: bfloat16 [131072, 1024], P(('hi', 'lo')), may hold values from -8 to 8
- key_rows: bfloat16 [131072, 1024], P(('hi', 'lo')), may hold values from -8 to 8
- value_rows: bfloat16 [131072, 1024], P(('hi', 'lo')), may hold values from -6 to 6
- doc_ids: int32 [131072], P(('hi', 'lo')), may hold values from 0 to 1023, never falling along the last dimension, each value on 1 to 512 neighbouring positions
- out_weight: bfloat16 [1024, 1024], replicated, may hold values from -0.1875 to 0.1875
- out_gain: float32 [1024], replicated, may hold values from 0.1 to 1.9
Outputs:
- mixed: bfloat16 [131072, 1024], P(('hi', 'lo'))
The draws below stay inside these ranges and needn't reach their ends.
Inputs may be any that keep to these rules, and one draw needn't show every extreme that they name: `doc_ids`: document numbers never fall along the sequence; each document holds 1 to 512 tokens.
All inputs are finite; a program needn't handle non-finite values.
Results may differ from the reference program's by a relative error of at most 0.009.
Values may be sent and summed in bfloat16 or wider, within the bound.
No kernel may reach another device: no remote copies, remote signals or barrier semaphores. Data moves between devices by JAX's collectives and lax.ppermute only.
A program may use at most 128 MiB of HBM per device.

```python
import math
from functools import reduce
import jax
import jax.numpy as jnp
import numpy as np
from jax import lax

HEADS = 8
HEAD = 128
BLOCK = 64
TOK_DEV = 512
D = 1024
TOKENS = 131072
DEVICES = 256


def draw_queries(key, part):
    values = jax.random.truncated_normal(jax.random.fold_in(key, 1), -6.0, 6.0, (TOKENS, HEADS * HEAD), jnp.float32)
    return values.astype(jnp.bfloat16)


def draw_key_rows(key, part):
    values = jax.random.truncated_normal(jax.random.fold_in(key, 2), -6.0, 6.0, (TOKENS, HEADS * HEAD), jnp.float32)
    return values.astype(jnp.bfloat16)


def block_scale(key, shape, pieces, low, largest):
    gain, own = 1.0, jax.random.fold_in(key, 6)
    for axis_at, parts in pieces:
        heights = jnp.exp(jax.random.uniform(jax.random.fold_in(own, axis_at), (parts,), jnp.float32, low / len(pieces), largest / len(pieces)))
        gain = gain * jnp.repeat(heights, shape[axis_at] // parts).reshape([-1 if axis == axis_at else 1 for axis in range(len(shape))])
    return gain


def split_up(amount, total, limit, lean):
    portions = [(1 << 20) // math.isqrt(grade ** lean) + 1 for grade in range(2, amount + 1)]
    rest, holding = total - limit - (amount - 1), [1] * (amount - 1)
    while rest > 0:
        candidates = [i for i in range(amount - 1) if holding[i] < limit]
        whole, left = sum([portions[i] for i in candidates]), rest
        for i in candidates:
            extra = min(limit - holding[i], max(1, left * portions[i] // whole), rest)
            holding[i] = holding[i] + extra
            rest = rest - extra
    return np.array([limit] + holding)


def uneven(stream_key, amount, total, reach, slope):
    if amount == 2:
        one = jax.random.randint(stream_key, (), max(1, total - reach), min(reach, total - 1) + 1)
        return jnp.stack([one, total - one])
    sizes = jnp.asarray(split_up(amount, total, reach, slope), jnp.int32)
    pairs = (amount - 1) // 2
    giver, taker = sizes[1:1 + 2 * pairs:2], sizes[2:2 + 2 * pairs:2]
    room = jnp.minimum(giver - 1, reach - taker)
    passed = jax.random.randint(jax.random.fold_in(stream_key, 1), (pairs,), 0, 1 << 20) % (room + 1)
    sizes = sizes.at[1:1 + 2 * pairs:2].set(giver - passed).at[2:2 + 2 * pairs:2].set(taker + passed)
    return sizes[jax.random.permutation(jax.random.fold_in(stream_key, 2), amount)]


def noise(key, dims, scale, bound, cuts=(), kind=jnp.bfloat16):
    level = block_scale(key, dims, cuts, -0.22, 0.18) if cuts else 1.0
    entries = jax.random.normal(key, dims, jnp.float32) * scale * level
    return jnp.minimum(jnp.maximum(entries, -bound), bound).astype(kind)


def setup_inputs(seed: int = 0) -> dict:
    arg_keys = jax.random.split(jax.random.key(seed), 7)
    queries = draw_queries(jax.random.fold_in(arg_keys[6], 71), 0)
    key_rows = draw_key_rows(jax.random.fold_in(arg_keys[6], 71), 0)
    value_rows = noise(arg_keys[2], (TOKENS, D), 1.0, 6.0, ((0, 256),))
    doc_ids = jnp.searchsorted(jnp.cumsum(uneven(arg_keys[3], TOKENS // 128, TOKENS, 512, 2)), jnp.arange(TOKENS), side="right").astype(jnp.int32)
    out_weight = noise(arg_keys[4], (D, D), D ** -0.5, 0.1875)
    out_gain = jnp.clip(1.0 + 0.18 * jax.random.normal(arg_keys[5], (D,), jnp.float32), 0.1, 1.9)
    return {"queries": queries, "key_rows": key_rows, "value_rows": value_rows, "doc_ids": doc_ids, "out_weight": out_weight, "out_gain": out_gain}


def attend(query_blocks, key_blocks, value_blocks, allowed):
    count, span, width_all = query_blocks.shape
    head_size = width_all // HEADS
    query_heads = query_blocks.reshape(count, span, HEADS, head_size).astype(jnp.float32)
    key_heads = key_blocks.reshape(count, -1, HEADS, head_size).astype(jnp.float32)
    value_heads = value_blocks.reshape(count, -1, HEADS, head_size).astype(jnp.float32)
    scores = jnp.einsum('bqhd,bkhd->bhqk', query_heads, key_heads) * head_size ** (-0.5)
    if allowed is not None:
        scores = jnp.where(allowed[:, None], scores, -jnp.inf)
    highest = lax.optimization_barrier(jnp.max(scores, axis=-1))
    weights = jnp.exp(scores - highest[..., None])
    totals = lax.optimization_barrier(jnp.sum(weights, axis=-1))
    rounded = lax.optimization_barrier(weights.astype(jnp.bfloat16))
    summed = jnp.einsum('bhqk,bkhd->bqhd', rounded.astype(jnp.float32), value_heads)
    partial_value = (summed / jnp.transpose(totals, (0, 2, 1))[..., None]).astype(jnp.bfloat16)
    return (partial_value, highest, totals)

def combine(results):
    peak = reduce(jnp.maximum, [item[1] for item in results])
    numer = None
    denom = None
    for partial_value, highest, totals in results:
        factor = totals * jnp.exp(highest - peak)
        term = jnp.transpose(factor, (0, 2, 1))[..., None] * partial_value.astype(jnp.float32)
        numer = term if numer is None else numer + term
        denom = factor if denom is None else denom + factor
    count, span = (numer.shape[0], numer.shape[1])
    merged = numer / jnp.transpose(denom, (0, 2, 1))[..., None]
    return merged.reshape(count, span, -1).astype(jnp.bfloat16)

def reference(queries, key_rows, value_rows, doc_ids, out_weight, out_gain):
    width_all = queries.shape[1]
    total_blocks = TOKENS // BLOCK
    blocks_dev = TOK_DEV // BLOCK
    local_bits = blocks_dev.bit_length() - 1
    all_bits = total_blocks.bit_length() - 1
    pairs = jnp.concatenate([key_rows, value_rows], axis=1).reshape(total_blocks, BLOCK, 2 * width_all)
    zero_block = jnp.zeros((1, BLOCK, 2 * width_all), pairs.dtype)
    padded = jnp.concatenate([zero_block, pairs, zero_block], axis=0)
    docs = (doc_ids + 1).reshape(total_blocks, BLOCK)
    zero_docs = jnp.zeros((1, BLOCK), jnp.int32)
    doc_pad = jnp.concatenate([zero_docs, docs, zero_docs], axis=0)
    query_blocks = queries.reshape(total_blocks, BLOCK, width_all)
    offsets = jnp.arange(BLOCK, dtype=jnp.int32)

    def one_device(device):
        local = jnp.arange(blocks_dev, dtype=jnp.int32)
        global_idx = (device * blocks_dev + local).astype(jnp.int32)
        parity = global_idx % 2
        beside = jnp.where(parity == 0, global_idx, global_idx + 2).astype(jnp.int32)
        columns = [global_idx + 1, beside]
        for bit_pos in range(local_bits):
            columns.append(jnp.bitwise_xor(global_idx, 1 << bit_pos) + 1)
        near_index = jnp.stack(columns, axis=1).astype(jnp.int32)
        near = padded[near_index].reshape(blocks_dev, -1, 2 * width_all)
        own_docs = docs[global_idx]
        side_docs = doc_pad[beside]
        relative = jnp.where(parity[:, None] == 0, offsets[None, :] - BLOCK, offsets[None, :] + BLOCK)
        band = jnp.abs(offsets[None, :, None] - relative[:, None, :]) <= BLOCK
        own_mask = own_docs[:, :, None] == own_docs[:, None, :]
        side_mask = (own_docs[:, :, None] == side_docs[:, None, :]) & band
        others = jnp.ones((blocks_dev, BLOCK, local_bits * BLOCK), jnp.bool_)
        allowed = jnp.concatenate([own_mask, side_mask, others], axis=-1)
        mine = query_blocks[global_idx]
        results = [attend(mine, near[..., :width_all], near[..., width_all:], allowed)]
        for bit_pos in range(local_bits, all_bits):
            far = pairs[jnp.bitwise_xor(global_idx, 1 << bit_pos).astype(jnp.int32)]
            results.append(attend(mine, far[..., :width_all], far[..., width_all:], None))
        return combine(results)
    attended = lax.map(one_device, jnp.arange(DEVICES, dtype=jnp.int32)).reshape(TOKENS, width_all)
    projected = jnp.dot(attended, out_weight, preferred_element_type=jnp.float32)
    scale = lax.rsqrt(lax.optimization_barrier(jnp.mean(projected * projected, axis=-1, keepdims=True)) + 1e-06)
    return (projected * scale * out_gain).astype(jnp.bfloat16)
```

```python
import functools
import math

import jax
import jax.numpy as jnp
import numpy as np
from jax import lax
from jax.experimental import pallas as pl
from jax.experimental.pallas import tpu as pltpu
from jax.sharding import PartitionSpec as P

HEADS = 8
HEAD = 128
BLOCK = 64
LOW = -1e30
VMEM_LIMIT = 48 * 1024 * 1024
SCALE = HEAD**-0.5 * math.log2(math.e)

NEIGHBOUR = [(z, z ^ 1) for z in range(8)]
PASS_ON = [(1, 2), (2, 1), (5, 6), (6, 5)]
TWO_HOPS = [(2, 0), (1, 3), (6, 4), (5, 7)]
FORWARD = [(3, 5), (7, 1), (0, 6), (4, 2)]
ASK = [(4, 1), (0, 5), (7, 2), (3, 6)]
ANSWER = [(b, a) for a, b in ASK]


def along_z(x, pairs):
    return lax.ppermute(x, "lo", [(2 * a + c, 2 * b + c) for a, b in pairs for c in (0, 1)])


def across(x, axis, mask):
    return lax.ppermute(x, axis, [(i, i ^ mask) for i in range(lax.axis_size(axis))])


def together(*values):
    return lax.optimization_barrier(values)


def scores(q, k):
    s = lax.dot_general(q, k, (((1,), (1,)), ((), ())), preferred_element_type=jnp.float32)
    return s * SCALE


def soft(s, v):
    peak = jnp.max(s, axis=-1, keepdims=True)
    p = jnp.exp2(s - peak)
    total = jnp.sum(p, axis=-1, keepdims=True)
    acc = jnp.dot(p.astype(jnp.bfloat16), v, preferred_element_type=jnp.float32)
    return acc, peak, total


def put_lane(ref, rows, h, value):
    old = ref[rows, :]
    lane = lax.broadcasted_iota(jnp.int32, old.shape, 1)
    ref[rows, :] = jnp.where(lane == h, value, jnp.where(h == 0, 0.0, old))


def get_lane(ref, rows, h):
    x = ref[rows, :].astype(jnp.float32)
    lane = lax.broadcasted_iota(jnp.int32, x.shape, 1)
    return jnp.sum(jnp.where(lane == h, x, 0.0), axis=-1, keepdims=True)


def cat(parts):
    return jnp.concatenate(parts, axis=0)


def near_kernel(flags, q, k, v, ck, cv, hk, hv, docq, dock, o, lse):
    h = pl.program_id(0)
    blocks = q.shape[0] // BLOCK
    first_core = flags[1] == 0

    def rows(i):
        return pl.ds(i * BLOCK, BLOCK)

    a = lax.broadcasted_iota(jnp.int32, (BLOCK, 2 * BLOCK), 0)
    b = lax.broadcasted_iota(jnp.int32, (BLOCK, 2 * BLOCK), 1)
    own = b >= BLOCK
    for i in range(blocks):
        if i == 0:
            side = [jnp.where(first_core, x[...], y[rows(blocks - 1), :]) for x, y in ((hk, ck), (hv, cv))]
        elif i == blocks - 1:
            side = [jnp.where(first_core, y[rows(0), :], x[...]) for x, y in ((hk, ck), (hv, cv))]
        else:
            j = i - 1 if i % 2 == 0 else i + 1
            side = [k[rows(j), :], v[rows(j), :]]
        local = [i, i ^ 1, i ^ 2, i ^ 4]
        keys = cat([side[0]] + [k[rows(j), :] for j in local] + [ck[rows(i), :]])
        values = cat([side[1]] + [v[rows(j), :] for j in local] + [cv[rows(i), :]])
        s = scores(q[rows(i), :], keys)
        band = b >= a if i % 2 == 0 else b <= a
        seen = (docq[rows(i), :] == dock[pl.ds(i, 1), :]) & (own | band)
        s = jnp.concatenate([jnp.where(seen, s[:, : 2 * BLOCK], LOW), s[:, 2 * BLOCK :]], axis=1)
        acc, peak, total = soft(s, values)
        o[rows(i), :] = acc * (1.0 / total)
        put_lane(lse, rows(i), h, peak + jnp.log2(total))


def merge(s, values, others):
    acc, peak, total = soft(s, values)
    top = peak
    for _, level in others:
        top = jnp.maximum(top, level)
    w = jnp.exp2(peak - top)
    denom = w * total
    numer = w * acc
    for out, level in others:
        w = jnp.exp2(level - top)
        denom = denom + w
        numer = numer + w * out
    return numer * (1.0 / denom), top, denom


def middle_kernel(q, *refs):
    pairs, (o_in, lse_in, o, lse) = refs[:-4], refs[-4:]
    h = pl.program_id(0)
    for i in range(q.shape[0] // BLOCK):
        rows = pl.ds(i * BLOCK, BLOCK)
        keys = cat([x[rows, :] for x in pairs[0::2]])
        values = cat([x[rows, :] for x in pairs[1::2]])
        s = scores(q[rows, :], keys)
        out, top, denom = merge(s, values, [(o_in[rows, :], get_lane(lse_in, rows, h))])
        o[rows, :] = out
        put_lane(lse, rows, h, top + jnp.log2(denom))


def answer_kernel(q, k, v, packed, lse):
    h = pl.program_id(0)
    for i in range(q.shape[0] // BLOCK):
        rows = pl.ds(i * BLOCK, BLOCK)
        acc, peak, total = soft(scores(q[rows, :], k[rows, :]), v[rows, :])
        packed[rows, pl.ds(pl.multiple_of(h * HEAD, HEAD), HEAD)] = (acc * (1.0 / total)).astype(jnp.bfloat16)
        level = peak + jnp.log2(total)
        old = lse[rows, :]
        lane = lax.broadcasted_iota(jnp.int32, old.shape, 1)
        old = jnp.where(h == 0, 0.0, old)
        for _ in range(3):
            part = level.astype(jnp.bfloat16).astype(jnp.float32)
            old = jnp.where(lane == h + 8 * _, part, old)
            level = level - part
        lse[rows, :] = old

    @pl.when(h == HEADS - 1)
    def _():
        packed[:, HEADS * HEAD :] = lse[...].astype(jnp.bfloat16)


def last_kernel(flags, q, ak, av, bk, bv, dk, dv, ck, cv, r_o, r_lse, o_in, lse_in, w, gain, *rest):
    out, att = rest[-2:]
    h = pl.program_id(0)
    inner = flags[0] == 1
    for i in range(q.shape[0] // BLOCK):
        rows = pl.ds(i * BLOCK, BLOCK)
        keys = cat([ck[rows, :], ak[rows, :], jnp.where(inner, bk[rows, :], dk[rows, :])])
        values = cat([cv[rows, :], av[rows, :], jnp.where(inner, bv[rows, :], dv[rows, :])])
        s = scores(q[rows, :], keys)
        lane = lax.broadcasted_iota(jnp.int32, s.shape, 1)
        s = jnp.where(inner | (lane >= BLOCK), s, LOW)
        x = r_lse[rows, :].astype(jnp.float32)
        lane = lax.broadcasted_iota(jnp.int32, x.shape, 1)
        level = jnp.sum(jnp.where((lane % 8 == h) & (lane < 24), x, 0.0), axis=-1, keepdims=True)
        level = jnp.where(inner, LOW, level)
        answered = (r_o[rows, :].astype(jnp.float32), level)
        held = (o_in[rows, :], get_lane(lse_in, rows, h))
        merged, _, _ = merge(s, values, [held, answered])
        att[rows, pl.ds(pl.multiple_of(h * HEAD, HEAD), HEAD)] = merged.astype(jnp.bfloat16)

    @pl.when(h == HEADS - 1)
    def _():
        projected = jnp.dot(att[...], w[...], preferred_element_type=jnp.float32)
        mean = jnp.mean(projected * projected, axis=-1, keepdims=True)
        out[...] = (projected * lax.rsqrt(mean + 1e-06) * gain[...]).astype(jnp.bfloat16)


def column(rows, first=0, row=0):
    return pl.BlockSpec((rows, HEAD), lambda h: (row, first + h))


def both(rows, row=0):
    return [column(rows, 0, row), column(rows, HEADS, row)]


def fixed(shape, index=(0, 0)):
    return pl.BlockSpec(shape, lambda h: index)


def scalars():
    return pl.BlockSpec(memory_space=pltpu.SMEM)


def call(kernel, name, in_specs, out_shape, out_specs, rows, keys, scratch=(), aliases=None, extra=0):
    flops = 4 * rows * keys * HEAD * HEADS + extra
    return pl.pallas_call(
        kernel,
        name=name,
        grid=(HEADS,),
        in_specs=in_specs,
        out_shape=out_shape,
        out_specs=out_specs,
        scratch_shapes=list(scratch),
        input_output_aliases=aliases or {},
        compiler_params=pltpu.CompilerParams(vmem_limit_bytes=VMEM_LIMIT),
        cost_estimate=pl.CostEstimate(
            flops=flops, bytes_accessed=rows * 1024 * 12, transcendentals=rows * keys * HEADS
        ),
    )


def carried(rows):
    return [
        jax.ShapeDtypeStruct((rows, HEADS * HEAD), jnp.float32),
        jax.ShapeDtypeStruct((rows, HEAD), jnp.float32),
    ]


def answer(asked, chunk, j):
    rows = chunk.shape[0]
    return call(
        answer_kernel, "answer",
        [column(rows, j * HEADS)] + both(rows),
        jax.ShapeDtypeStruct((rows, HEADS * HEAD + HEAD), jnp.bfloat16),
        fixed((rows, HEADS * HEAD + HEAD)),
        rows, BLOCK, scratch=[pltpu.VMEM((rows, HEAD), jnp.float32)],
    )(asked, chunk, chunk)


def last(flags, queries, a, b, d, c, r, o, lse, weight, gain, j, out):
    rows, tokens = a.shape[0], queries.shape[0]
    specs = (
        [scalars(), column(rows, 0, j)] + both(rows) * 4
        + [column(rows), fixed((rows, HEAD), (0, HEADS)), column(rows, 0, j), fixed((rows, HEAD), (j, 0))]
        + [fixed(weight.shape), fixed(gain.shape)]
    )
    args = [flags, queries, a, a, b, b, d, d, c, c, r, r, o, lse, weight, gain]
    if out is not None:
        specs.append(pl.BlockSpec(memory_space=pl.ANY))
        args.append(out)
    return call(
        last_kernel, "last", specs,
        jax.ShapeDtypeStruct((tokens, HEADS * HEAD), jnp.bfloat16),
        fixed((rows, HEADS * HEAD), (j, 0)),
        rows, 3 * BLOCK, scratch=[pltpu.VMEM((rows, HEADS * HEAD), jnp.bfloat16)],
        aliases={len(args) - 1: 0} if out is not None else None,
        extra=2 * rows * weight.size,
    )(*args)


def body(queries, key_rows, value_rows, doc_ids, out_weight, out_gain):
    tokens = queries.shape[0]
    half = tokens // 2
    blocks = tokens // BLOCK
    lo = lax.axis_index("lo")
    z, core = lo // 2, lo % 2
    inner = ((z % 4) == 1) | ((z % 4) == 2)
    flags = jnp.stack([inner.astype(jnp.int32), core.astype(jnp.int32)])
    q2 = jnp.concatenate([queries[:half], queries[half:]], axis=1)
    x1 = jnp.concatenate([key_rows[:half], value_rows[:half]], axis=1)
    x2 = jnp.concatenate([key_rows[half:], value_rows[half:]], axis=1)

    a1 = along_z(x1, NEIGHBOUR)
    d1 = along_z(jnp.where(inner, x1, q2), ASK + TWO_HOPS)
    x = jnp.concatenate([x1, x2], axis=0)
    cores = across(x, "lo", 1)

    docs = doc_ids + 1
    first_core = core == 0
    size = lax.axis_size("hi") * lax.axis_size("lo")
    edge = [(d, d + 1) for d in range(1, size - 1, 2)] + [(d, d - 1) for d in range(2, size, 2)]
    halo = lax.ppermute(jnp.where(first_core, x[:BLOCK], x[tokens - BLOCK :]), ("hi", "lo"), edge)
    ends = jnp.stack([docs[:BLOCK], docs[tokens - BLOCK :]])
    doc_halo = lax.ppermute(jnp.where(first_core, ends[0], ends[1]), ("hi", "lo"), edge)
    doc_core = across(jnp.where(first_core, ends[1], ends[0]), "lo", 1)

    own = docs.reshape(blocks, BLOCK)
    before = jnp.where(first_core, doc_halo, doc_core)[None]
    after = jnp.where(first_core, doc_core, doc_halo)[None]
    padded = jnp.concatenate([before, own, after], axis=0)
    side = [i if i % 2 == 0 else i + 2 for i in range(blocks)]
    beside = jnp.concatenate([padded[i : i + 1] for i in side], axis=0)
    doc_keys = jnp.concatenate([beside, own], axis=1)
    doc_queries = jnp.broadcast_to(docs[:, None], (tokens, HEAD))

    cores, halo, xs = together(cores, halo, x)
    y1 = across(xs, "hi", 1)
    w1 = across(xs, "hi", 4)
    o, lse = call(
        near_kernel, "near",
        [scalars(), column(tokens), column(tokens), column(tokens)]
        + both(tokens) + both(BLOCK) + [fixed((tokens, HEAD)), fixed((blocks, HEAD))],
        carried(tokens), [column(tokens), fixed((tokens, HEAD))], tokens, 6 * BLOCK,
    )(flags, queries, key_rows, value_rows, cores, cores, halo, halo, doc_queries, doc_keys)

    a1, d1, x2 = together(a1, d1, x2)
    a2 = along_z(x2, NEIGHBOUR)
    e1 = along_z(jnp.where(inner, x2, d1), FORWARD + TWO_HOPS)
    r1 = along_z(answer(d1, a1, 0), ANSWER)
    b1 = along_z(a1, PASS_ON)
    w1, xs = together(w1, xs)
    w2 = across(xs, "hi", 8)
    r1, xs = together(r1, xs)
    y2 = across(xs, "hi", 2)

    a2, e1, r1 = together(a2, e1, r1)
    c2 = along_z(e1, FORWARD)
    b2 = along_z(a2, PASS_ON)
    r2 = along_z(answer(d1, a2, 1), ANSWER)

    o, lse = call(
        middle_kernel, "middle",
        [column(tokens)] + both(tokens) * 4 + [column(tokens), fixed((tokens, HEAD))],
        carried(tokens), [column(tokens), fixed((tokens, HEAD))], tokens, 4 * BLOCK,
    )(queries, y1, y1, w1, w1, w2, w2, y2, y2, o, lse)
    gain = out_gain[None]
    out = last(flags, queries, a1, b1, d1, e1, r1, o, lse, out_weight, gain, 0, None)
    return last(flags, queries, a2, b2, e1, c2, r2, o, lse, out_weight, gain, 1, out)


def solution(mesh):
    rows = P(("hi", "lo"), None)
    return jax.shard_map(
        body,
        mesh=mesh,
        in_specs=(rows, rows, rows, P(("hi", "lo")), P(), P()),
        out_specs=rows,
        check_vma=False,
    )
```

```python
import functools
import math

import jax
import jax.numpy as jnp
import numpy as np
from jax import lax
from jax.experimental import pallas as pl
from jax.experimental.pallas import tpu as pltpu
from jax.sharding import PartitionSpec as P

HEADS = 8
HEAD = 128
BLOCK = 64
LOW = -1e30
VMEM_LIMIT = 48 * 1024 * 1024
SCALE = HEAD**-0.5 * math.log2(math.e)

NEIGHBOUR = [(z, z ^ 1) for z in range(8)]
PASS_ON = [(1, 2), (2, 1), (5, 6), (6, 5)]
TWO_HOPS = [(2, 0), (1, 3), (6, 4), (5, 7)]
FORWARD = [(3, 5), (7, 1), (0, 6), (4, 2)]
ASK = [(4, 1), (0, 5), (7, 2), (3, 6)]
ANSWER = [(b, a) for a, b in ASK]


def along_z(x, pairs):
    return lax.ppermute(x, "lo", [(2 * a + c, 2 * b + c) for a, b in pairs for c in (0, 1)])


def across(x, axis, mask):
    return lax.ppermute(x, axis, [(i, i ^ mask) for i in range(lax.axis_size(axis))])


def together(*values):
    return lax.optimization_barrier(values)


def scores(q, k):
    s = lax.dot_general(q, k, (((1,), (1,)), ((), ())), preferred_element_type=jnp.float32)
    return s * SCALE


def cat(parts):
    return jnp.concatenate(parts, axis=0)


def blockwise(q, k):
    return cat([scores(q[i * BLOCK : (i + 1) * BLOCK], keys) for i, keys in enumerate(k)])


def weighted(p, v):
    p = p.astype(jnp.bfloat16)
    return cat(
        [
            jnp.dot(p[i * BLOCK : (i + 1) * BLOCK], values, preferred_element_type=jnp.float32)
            for i, values in enumerate(v)
        ]
    )


def rows_of(x, i):
    return x[i * BLOCK : (i + 1) * BLOCK]


def per_block(arrays, n):
    return [cat([rows_of(x, i) for x in arrays]) for i in range(n)]


def soft(s, v):
    peak = jnp.max(s, axis=-1, keepdims=True)
    p = jnp.exp2(s - peak)
    total = jnp.sum(p, axis=-1, keepdims=True)
    return weighted(p, v), peak, total


def put_lanes(ref, first, columns, old=None):
    old = jnp.where(first == 0, 0.0, ref[...]) if old is None else old
    lane = lax.broadcasted_iota(jnp.int32, old.shape, 1)
    for g, value in enumerate(columns):
        old = jnp.where(lane == first + g, value, old)
    ref[...] = old


def get_lane(x, h):
    lane = lax.broadcasted_iota(jnp.int32, x.shape, 1)
    return jnp.sum(jnp.where(lane == h, x, 0.0), axis=-1, keepdims=True)


def heads_of(ref):
    return [slice(g * HEAD, (g + 1) * HEAD) for g in range(ref.shape[1] // HEAD)]


def near_kernel(flags, q, k, v, ck, cv, hk, hv, docq, dock, o, lse):
    n = q.shape[0] // BLOCK
    first_core = flags[1] == 0
    a = lax.broadcasted_iota(jnp.int32, (BLOCK, 2 * BLOCK), 0)
    b = lax.broadcasted_iota(jnp.int32, (BLOCK, 2 * BLOCK), 1)
    masks = [(b >= BLOCK) | (b >= a), (b >= BLOCK) | (b <= a)]
    seen = cat([(rows_of(docq[...], i) == dock[i : i + 1, :]) & masks[i % 2] for i in range(n)])

    def gather(x, edge, core):
        first = jnp.where(first_core, edge, rows_of(core, n - 1))
        final = jnp.where(first_core, rows_of(core, 0), edge)
        side = [first] + [rows_of(x, i - 1 if i % 2 == 0 else i + 1) for i in range(1, n - 1)] + [final]
        return [
            cat([side[i]] + [rows_of(x, j) for j in (i, i ^ 1, i ^ 2, i ^ 4)] + [rows_of(core, i)])
            for i in range(n)
        ]

    levels = []
    for at in heads_of(q):
        s = blockwise(q[:, at], gather(k[:, at], hk[:, at], ck[:, at]))
        s = jnp.concatenate([jnp.where(seen, s[:, : 2 * BLOCK], LOW), s[:, 2 * BLOCK :]], axis=1)
        acc, peak, total = soft(s, gather(v[:, at], hv[:, at], cv[:, at]))
        o[:, at] = acc * (1.0 / total)
        levels.append(peak + jnp.log2(total))
    put_lanes(lse, pl.program_id(0) * len(levels), levels)


def merge(s, values, others):
    acc, peak, total = soft(s, values)
    top = peak
    for _, level in others:
        top = jnp.maximum(top, level)
    w = jnp.exp2(peak - top)
    denom = w * total
    weights = [w]
    for _, level in others:
        weights.append(jnp.exp2(level - top))
        denom = denom + weights[-1]
    share = 1.0 / denom
    numer = (w * share) * acc
    for (out, _), w in zip(others, weights[1:]):
        numer = numer + (w * share) * out
    return numer, top, denom


def middle_kernel(flags, q, *refs):
    far, rest = refs[:8], refs[8:]
    (a1k, a1v, a2k, a2v, b1k, b1v, d1k, d1v, e1k, e1v, o_in, lse_in, o, lse) = rest
    inner = flags[0] == 1
    half = q.shape[0] // 2
    n = half // BLOCK
    outs = [[], []]
    first = pl.program_id(0) * len(heads_of(q))
    for j in range(2):
        rows = slice(j * half, (j + 1) * half)
        old = lse_in[rows, :]
        for g, at in enumerate(heads_of(q)):

            def sets(far, a1, a2, b1, d1, e1):
                arrays = [x[rows, at] for x in far]
                if j == 0:
                    arrays += [a1[:, at], jnp.where(inner, b1[:, at], d1[:, at]), e1[:, at], e1[:, at]]
                else:
                    arrays += [a2[:, at], e1[:, at]]
                return per_block(arrays, n)

            s = blockwise(q[rows, at], sets(far[0::2], a1k, a2k, b1k, d1k, e1k))
            tail = s[:, 6 * BLOCK :] if j == 0 else s[:, 4 * BLOCK :]
            lane = lax.broadcasted_iota(jnp.int32, tail.shape, 1)
            seen = (inner & (lane < BLOCK)) if j == 0 else ((lane < BLOCK) | jnp.logical_not(inner))
            s = jnp.concatenate([s[:, : s.shape[1] - 2 * BLOCK], jnp.where(seen, tail, LOW)], axis=1)
            values = sets(far[1::2], a1v, a2v, b1v, d1v, e1v)
            out, top, denom = merge(s, values, [(o_in[rows, at], get_lane(old, first + g))])
            o[rows, at] = out
            outs[j].append(top + jnp.log2(denom))
    put_lanes(lse, first, [cat(pair) for pair in zip(*outs)])


def answer_kernel(q, k, v, packed, lse):
    n = q.shape[0] // BLOCK
    heads = heads_of(q)
    first = pl.program_id(0) * len(heads)
    old = jnp.where(first == 0, 0.0, lse[...])
    lane = lax.broadcasted_iota(jnp.int32, old.shape, 1)
    for g, at in enumerate(heads):
        acc, peak, total = soft(blockwise(q[:, at], per_block([k[:, at]], n)), per_block([v[:, at]], n))
        start = pl.multiple_of((first + g) * HEAD, HEAD)
        packed[:, pl.ds(start, HEAD)] = (acc * (1.0 / total)).astype(jnp.bfloat16)
        level = peak + jnp.log2(total)
        for part_at in range(3):
            part = level.astype(jnp.bfloat16).astype(jnp.float32)
            old = jnp.where(lane == first + g + HEADS * part_at, part, old)
            level = level - part
    lse[...] = old

    @pl.when(pl.program_id(0) == pl.num_programs(0) - 1)
    def _():
        packed[:, HEADS * HEAD :] = lse[...].astype(jnp.bfloat16)


def finish(att, w, gain, out):
    projected = jnp.dot(att[...], w[...], preferred_element_type=jnp.float32)
    mean = jnp.mean(projected * projected, axis=-1, keepdims=True)
    out[...] = (projected * lax.rsqrt(mean + 1e-06) * gain[...]).astype(jnp.bfloat16)


def last_kernel(flags, *refs):
    late = None
    if len(refs) > 8:
        late, refs = refs[:5], refs[5:]
    r_o, r_lse, o_in, lse_in, w, gain = refs[:6]
    out, att = refs[-2:]
    heads = heads_of(o_in)
    first = pl.program_id(0) * len(heads)
    inner = flags[0] == 1
    x = r_lse[...].astype(jnp.float32)
    lane = lax.broadcasted_iota(jnp.int32, x.shape, 1)
    old = lse_in[...]
    for g, at in enumerate(heads):
        mine = ((lane & (HEADS - 1)) == first + g) & (lane < 3 * HEADS)
        level = jnp.sum(jnp.where(mine, x, 0.0), axis=-1, keepdims=True)
        level = jnp.where(inner, LOW, level)
        answered = (r_o[:, at].astype(jnp.float32), level)
        held = (o_in[:, at], get_lane(old, first + g))
        if late is None:
            top = jnp.maximum(level, held[1])
            ways = [jnp.exp2(l - top) for _, l in (held, answered)]
            share = 1.0 / (ways[0] + ways[1])
            merged = (ways[0] * share) * held[0] + (ways[1] * share) * answered[0]
        else:
            q, bk, bv, ck, cv = late
            n = q.shape[0] // BLOCK
            s = blockwise(q[:, at], per_block([bk[:, at], ck[:, at]], n))
            s = jnp.where(inner, s, LOW)
            merged, _, _ = merge(s, per_block([bv[:, at], cv[:, at]], n), [held, answered])
        att[:, pl.ds(pl.multiple_of((first + g) * HEAD, HEAD), HEAD)] = merged.astype(jnp.bfloat16)

    @pl.when(pl.program_id(0) == pl.num_programs(0) - 1)
    def _():
        finish(att, w, gain, out)


def column(rows, heads, first=0, row=0):
    return pl.BlockSpec((rows, heads * HEAD), lambda h: (row, first // heads + h))


def both(rows, heads, row=0):
    return [column(rows, heads, 0, row), column(rows, heads, HEADS, row)]


def fixed(shape, index=(0, 0)):
    return pl.BlockSpec(shape, lambda h: index)


def scalars():
    return pl.BlockSpec(memory_space=pltpu.SMEM)


def call(kernel, name, heads, in_specs, out_shape, out_specs, rows, keys, scratch=(), aliases=None, extra=0):
    flops = 4 * rows * keys * HEAD * HEADS + extra
    return pl.pallas_call(
        kernel,
        name=name,
        grid=(HEADS // heads,),
        in_specs=in_specs,
        out_shape=out_shape,
        out_specs=out_specs,
        scratch_shapes=list(scratch),
        input_output_aliases=aliases or {},
        compiler_params=pltpu.CompilerParams(vmem_limit_bytes=VMEM_LIMIT),
        cost_estimate=pl.CostEstimate(
            flops=flops, bytes_accessed=rows * 1024 * 12, transcendentals=rows * keys * HEADS
        ),
    )


def carried(rows):
    return [
        jax.ShapeDtypeStruct((rows, HEADS * HEAD), jnp.float32),
        jax.ShapeDtypeStruct((rows, HEAD), jnp.float32),
    ]


def near(flags, q, k, v, cores, halo, doc_queries, doc_keys, heads=2):
    tokens, blocks = q.shape[0], doc_keys.shape[0]
    return call(
        near_kernel, "near", heads,
        [scalars(), column(tokens, heads), column(tokens, heads), column(tokens, heads)]
        + both(tokens, heads) + both(BLOCK, heads) + [fixed((tokens, HEAD)), fixed((blocks, HEAD))],
        carried(tokens), [column(tokens, heads), fixed((tokens, HEAD))], tokens, 6 * BLOCK,
    )(flags, q, k, v, cores, cores, halo, halo, doc_queries, doc_keys)


def middle(flags, q, far, a1, a2, b1, d1, e1, o, lse, heads=2):
    tokens = q.shape[0]
    whole, half = column(tokens, heads), both(tokens // 2, heads)
    return call(
        middle_kernel, "middle", heads,
        [scalars(), whole] + both(tokens, heads) * len(far) + half * 5 + [whole, fixed((tokens, HEAD))],
        carried(tokens), [whole, fixed((tokens, HEAD))], tokens, 7 * BLOCK,
    )(flags, q, *[x for x in [*far, a1, a2, b1, d1, e1] for _ in (0, 1)], o, lse)


def answer(asked, chunk, j, heads=4):
    rows = chunk.shape[0]
    return call(
        answer_kernel, "answer", heads,
        [column(rows, heads, j * HEADS)] + both(rows, heads),
        jax.ShapeDtypeStruct((rows, HEADS * HEAD + HEAD), jnp.bfloat16),
        fixed((rows, HEADS * HEAD + HEAD)),
        rows, BLOCK, scratch=[pltpu.VMEM((rows, HEAD), jnp.float32)],
    )(asked, chunk, chunk)


def last(flags, late, r, o, lse, weight, gain, j, out, heads=4):
    rows, tokens = r.shape[0], o.shape[0]
    specs, args = [scalars()], [flags]
    if late:
        queries, b, c = late
        specs += [column(rows, heads, 0, j)] + both(rows, heads) * 2
        args += [queries, b, b, c, c]
    specs += [column(rows, heads), fixed((rows, HEAD), (0, HEADS)), column(rows, heads, 0, j)]
    specs += [fixed((rows, HEAD), (j, 0)), fixed(weight.shape), fixed(gain.shape)]
    args += [r, r, o, lse, weight, gain]
    if out is not None:
        specs.append(pl.BlockSpec(memory_space=pl.ANY))
        args.append(out)
    return call(
        last_kernel, "last", heads, specs,
        jax.ShapeDtypeStruct((tokens, HEADS * HEAD), jnp.bfloat16),
        fixed((rows, HEADS * HEAD), (j, 0)),
        rows, 2 * BLOCK, scratch=[pltpu.VMEM((rows, HEADS * HEAD), jnp.bfloat16)],
        aliases={len(args) - 1: 0} if out is not None else None,
        extra=2 * rows * weight.size,
    )(*args)


def doc_rows(docs):
    digits = jnp.concatenate([docs // 32, docs % 32]).astype(jnp.bfloat16)
    return jnp.zeros((16, 2 * HEADS * HEAD), jnp.bfloat16).at[0, : digits.size].set(digits)


def docs_of(row, tokens):
    digits = row[: 2 * tokens].astype(jnp.int32)
    return digits[:tokens] * 32 + digits[tokens:]


def body(queries, key_rows, value_rows, doc_ids, out_weight, out_gain):
    tokens = queries.shape[0]
    half = tokens // 2
    blocks = tokens // BLOCK
    lo = lax.axis_index("lo")
    z, core = lo // 2, lo % 2
    inner = ((z % 4) == 1) | ((z % 4) == 2)
    first_core = core == 0
    flags = jnp.stack([inner.astype(jnp.int32), core])

    x1 = jnp.concatenate([key_rows[:half], value_rows[:half]], axis=1)
    a1 = along_z(x1, NEIGHBOUR)
    q2 = jnp.concatenate([queries[:half], queries[half:]], axis=1)
    d1 = along_z(jnp.where(inner, x1, q2), ASK + TWO_HOPS)
    x2 = jnp.concatenate([key_rows[half:], value_rows[half:]], axis=1)
    x = jnp.concatenate([key_rows, value_rows], axis=1)
    y1 = across(x, "hi", 1)
    w1 = across(x, "hi", 4)
    docs = doc_ids + 1
    numbers = doc_rows(docs)
    cores = across(jnp.concatenate([x, numbers], axis=0), "lo", 1)

    a1, d1, x2, x, y1, w1 = together(a1, d1, x2, x, y1, w1)
    a2 = along_z(x2, NEIGHBOUR)
    e1 = along_z(jnp.where(inner, x2, d1), FORWARD + TWO_HOPS)
    b1 = along_z(a1, PASS_ON)
    y2 = across(x, "hi", 2)
    w2 = across(x, "hi", 8)
    answers = answer(d1, a1, 0)
    ends = jnp.where(first_core, x[:BLOCK], x[tokens - BLOCK :])
    ends = jnp.concatenate([ends, numbers], axis=0)

    a2, e1, b1, y2, w2, answers, ends = together(a2, e1, b1, y2, w2, answers, ends)
    r1 = along_z(answers, ANSWER)
    c2 = along_z(e1, FORWARD)
    b2 = along_z(a2, PASS_ON)
    r2 = along_z(answer(d1, a2, 1), ANSWER)
    size = lax.axis_size("hi") * lax.axis_size("lo")
    edge = [(d, d + 1) for d in range(1, size - 1, 2)] + [(d, d - 1) for d in range(2, size, 2)]
    halo = lax.ppermute(ends, ("hi", "lo"), edge)

    core_docs = docs_of(cores[tokens], tokens)
    halo_docs = docs_of(halo[BLOCK], tokens)
    own = docs.reshape(blocks, BLOCK)
    before = jnp.where(first_core, halo_docs, core_docs)[tokens - BLOCK :]
    after = jnp.where(first_core, core_docs, halo_docs)[:BLOCK]
    padded = jnp.concatenate([before[None], own, after[None]], axis=0)
    side = [i if i % 2 == 0 else i + 2 for i in range(blocks)]
    beside = jnp.concatenate([padded[i : i + 1] for i in side], axis=0)
    doc_keys = jnp.concatenate([beside, own], axis=1)
    doc_queries = jnp.broadcast_to(docs[:, None], (tokens, HEAD))
    o, lse = near(flags, queries, key_rows, value_rows, cores, halo, doc_queries, doc_keys)
    o, lse = middle(flags, queries, [y1, y2, w1, w2], a1, a2, b1, d1, e1, o, lse)
    gain = out_gain[None]
    out = last(flags, None, r1, o, lse, out_weight, gain, 0, None)
    return last(flags, (queries, b2, c2), r2, o, lse, out_weight, gain, 1, out)


def solution(mesh):
    rows = P(("hi", "lo"), None)
    return jax.shard_map(
        body,
        mesh=mesh,
        in_specs=(rows, rows, rows, P(("hi", "lo")), P(), P()),
        out_specs=rows,
        check_vma=False,
    )
```

```python
import functools
import math

import jax
import jax.numpy as jnp
import numpy as np
from jax import lax
from jax.experimental import pallas as pl
from jax.experimental.pallas import tpu as pltpu
from jax.sharding import PartitionSpec as P

HEADS = 8
HEAD = 128
BLOCK = 64
LOW = -1e30
VMEM_LIMIT = 48 * 1024 * 1024
SCALE = HEAD**-0.5 * math.log2(math.e)

NEIGHBOUR = [(z, z ^ 1) for z in range(8)]
PASS_ON = [(1, 2), (2, 1), (5, 6), (6, 5)]
TWO_HOPS = [(2, 0), (1, 3), (6, 4), (5, 7)]
FORWARD = [(3, 5), (7, 1), (0, 6), (4, 2)]
ASK = [(4, 1), (0, 5), (7, 2), (3, 6)]
ANSWER = [(b, a) for a, b in ASK]


def along_z(x, pairs):
    return lax.ppermute(x, "lo", [(2 * a + c, 2 * b + c) for a, b in pairs for c in (0, 1)])


def across(x, axis, mask):
    return lax.ppermute(x, axis, [(i, i ^ mask) for i in range(lax.axis_size(axis))])


def together(*values):
    return lax.optimization_barrier(values)


def scores(q, k):
    s = lax.dot_general(q, k, (((1,), (1,)), ((), ())), preferred_element_type=jnp.float32)
    return s * SCALE


def cat(parts):
    return jnp.concatenate(parts, axis=0)


def blockwise(q, k):
    return cat([scores(q[i * BLOCK : (i + 1) * BLOCK], keys) for i, keys in enumerate(k)])


def weighted(p, v):
    p = p.astype(jnp.bfloat16)
    return cat(
        [
            jnp.dot(p[i * BLOCK : (i + 1) * BLOCK], values, preferred_element_type=jnp.float32)
            for i, values in enumerate(v)
        ]
    )


def rows_of(x, i):
    return x[i * BLOCK : (i + 1) * BLOCK]


def per_block(arrays, n):
    return [cat([rows_of(x, i) for x in arrays]) for i in range(n)]


def soft(s, v):
    peak = jnp.max(s, axis=-1, keepdims=True)
    p = jnp.exp2(s - peak)
    total = jnp.sum(p, axis=-1, keepdims=True)
    return weighted(p, v), peak, total


def put_lanes(ref, first, columns, old=None):
    old = jnp.where(first == 0, 0.0, ref[...]) if old is None else old
    lane = lax.broadcasted_iota(jnp.int32, old.shape, 1)
    for g, value in enumerate(columns):
        old = jnp.where(lane == first + g, value, old)
    ref[...] = old


def get_lane(x, h):
    lane = lax.broadcasted_iota(jnp.int32, x.shape, 1)
    return jnp.sum(jnp.where(lane == h, x, 0.0), axis=-1, keepdims=True)


def heads_of(ref):
    return [slice(g * HEAD, (g + 1) * HEAD) for g in range(ref.shape[1] // HEAD)]


def near_kernel(flags, q, k, v, ck, cv, hk, hv, docq, dock, o, lse):
    n = q.shape[0] // BLOCK
    first_core = flags[1] == 0
    a = lax.broadcasted_iota(jnp.int32, (BLOCK, 2 * BLOCK), 0)
    b = lax.broadcasted_iota(jnp.int32, (BLOCK, 2 * BLOCK), 1)
    masks = [(b >= BLOCK) | (b >= a), (b >= BLOCK) | (b <= a)]
    seen = cat([(rows_of(docq[...], i) == dock[i : i + 1, :]) & masks[i % 2] for i in range(n)])

    def gather(x, edge, core):
        first = jnp.where(first_core, edge, rows_of(core, n - 1))
        final = jnp.where(first_core, rows_of(core, 0), edge)
        side = [first] + [rows_of(x, i - 1 if i % 2 == 0 else i + 1) for i in range(1, n - 1)] + [final]
        return [
            cat([side[i]] + [rows_of(x, j) for j in (i, i ^ 1, i ^ 2, i ^ 4)] + [rows_of(core, i)])
            for i in range(n)
        ]

    levels = []
    for at in heads_of(q):
        s = blockwise(q[:, at], gather(k[:, at], hk[:, at], ck[:, at]))
        s = jnp.concatenate([jnp.where(seen, s[:, : 2 * BLOCK], LOW), s[:, 2 * BLOCK :]], axis=1)
        acc, peak, total = soft(s, gather(v[:, at], hv[:, at], cv[:, at]))
        o[:, at] = acc * (1.0 / total)
        levels.append(peak + jnp.log2(total))
    put_lanes(lse, pl.program_id(0) * len(levels), levels)


def merge(s, values, others):
    acc, peak, total = soft(s, values)
    top = peak
    for _, level in others:
        top = jnp.maximum(top, level)
    w = jnp.exp2(peak - top)
    denom = w * total
    weights = [w]
    for _, level in others:
        weights.append(jnp.exp2(level - top))
        denom = denom + weights[-1]
    share = 1.0 / denom
    numer = (w * share) * acc
    for (out, _), w in zip(others, weights[1:]):
        numer = numer + (w * share) * out
    return numer, top, denom


def middle_kernel(flags, q, *refs):
    far, rest = refs[:8], refs[8:]
    (a1k, a1v, a2k, a2v, b1k, b1v, d1k, d1v, e1k, e1v, o_in, lse_in, o, lse) = rest
    inner = flags[0] == 1
    half = q.shape[0] // 2
    n = half // BLOCK
    outs = [[], []]
    first = pl.program_id(0) * len(heads_of(q))
    for j in range(2):
        rows = slice(j * half, (j + 1) * half)
        old = lse_in[rows, :]
        for g, at in enumerate(heads_of(q)):

            def sets(far, a1, a2, b1, d1, e1):
                arrays = [x[rows, at] for x in far]
                if j == 0:
                    arrays += [a1[:, at], jnp.where(inner, b1[:, at], d1[:, at]), e1[:, at], e1[:, at]]
                else:
                    arrays += [a2[:, at], e1[:, at]]
                return per_block(arrays, n)

            s = blockwise(q[rows, at], sets(far[0::2], a1k, a2k, b1k, d1k, e1k))
            tail = s[:, 6 * BLOCK :] if j == 0 else s[:, 4 * BLOCK :]
            lane = lax.broadcasted_iota(jnp.int32, tail.shape, 1)
            seen = (inner & (lane < BLOCK)) if j == 0 else ((lane < BLOCK) | jnp.logical_not(inner))
            s = jnp.concatenate([s[:, : s.shape[1] - 2 * BLOCK], jnp.where(seen, tail, LOW)], axis=1)
            values = sets(far[1::2], a1v, a2v, b1v, d1v, e1v)
            out, top, denom = merge(s, values, [(o_in[rows, at], get_lane(old, first + g))])
            o[rows, at] = out
            outs[j].append(top + jnp.log2(denom))
    put_lanes(lse, first, [cat(pair) for pair in zip(*outs)])


def answer_kernel(q, k, v, packed, lse):
    n = q.shape[0] // BLOCK
    heads = heads_of(q)
    first = pl.program_id(0) * len(heads)
    old = jnp.where(first == 0, 0.0, lse[...])
    lane = lax.broadcasted_iota(jnp.int32, old.shape, 1)
    for g, at in enumerate(heads):
        acc, peak, total = soft(blockwise(q[:, at], per_block([k[:, at]], n)), per_block([v[:, at]], n))
        start = pl.multiple_of((first + g) * HEAD, HEAD)
        packed[:, pl.ds(start, HEAD)] = (acc * (1.0 / total)).astype(jnp.bfloat16)
        level = peak + jnp.log2(total)
        for part_at in range(3):
            part = level.astype(jnp.bfloat16).astype(jnp.float32)
            old = jnp.where(lane == first + g + HEADS * part_at, part, old)
            level = level - part
    lse[...] = old

    @pl.when(pl.program_id(0) == pl.num_programs(0) - 1)
    def _():
        packed[:, HEADS * HEAD :] = lse[...].astype(jnp.bfloat16)


def finish(att, w, gain, out):
    projected = jnp.dot(att[...], w[...], preferred_element_type=jnp.float32)
    mean = jnp.mean(projected * projected, axis=-1, keepdims=True)
    out[...] = (projected * lax.rsqrt(mean + 1e-06) * gain[...]).astype(jnp.bfloat16)


def last_kernel(flags, *refs):
    late = None
    if len(refs) > 8:
        late, refs = refs[:5], refs[5:]
    r_o, r_lse, o_in, lse_in, w, gain = refs[:6]
    out, att = refs[-2:]
    heads = heads_of(o_in)
    first = pl.program_id(0) * len(heads)
    inner = flags[0] == 1
    x = r_lse[...].astype(jnp.float32)
    lane = lax.broadcasted_iota(jnp.int32, x.shape, 1)
    old = lse_in[...]
    for g, at in enumerate(heads):
        mine = ((lane & (HEADS - 1)) == first + g) & (lane < 3 * HEADS)
        level = jnp.sum(jnp.where(mine, x, 0.0), axis=-1, keepdims=True)
        level = jnp.where(inner, LOW, level)
        answered = (r_o[:, at].astype(jnp.float32), level)
        held = (o_in[:, at], get_lane(old, first + g))
        if late is None:
            top = jnp.maximum(level, held[1])
            ways = [jnp.exp2(l - top) for _, l in (held, answered)]
            share = 1.0 / (ways[0] + ways[1])
            merged = (ways[0] * share) * held[0] + (ways[1] * share) * answered[0]
        else:
            q, bk, bv, ck, cv = late
            n = q.shape[0] // BLOCK
            s = blockwise(q[:, at], per_block([bk[:, at], ck[:, at]], n))
            s = jnp.where(inner, s, LOW)
            merged, _, _ = merge(s, per_block([bv[:, at], cv[:, at]], n), [held, answered])
        att[:, pl.ds(pl.multiple_of((first + g) * HEAD, HEAD), HEAD)] = merged.astype(jnp.bfloat16)

    @pl.when(pl.program_id(0) == pl.num_programs(0) - 1)
    def _():
        finish(att, w, gain, out)


def column(rows, heads, first=0, row=0):
    return pl.BlockSpec((rows, heads * HEAD), lambda h: (row, first // heads + h))


def both(rows, heads, row=0):
    return [column(rows, heads, 0, row), column(rows, heads, HEADS, row)]


def fixed(shape, index=(0, 0)):
    return pl.BlockSpec(shape, lambda h: index)


def scalars():
    return pl.BlockSpec(memory_space=pltpu.SMEM)


def call(kernel, name, heads, in_specs, out_shape, out_specs, rows, keys, scratch=(), aliases=None, extra=0):
    flops = 4 * rows * keys * HEAD * HEADS + extra
    return pl.pallas_call(
        kernel,
        name=name,
        grid=(HEADS // heads,),
        in_specs=in_specs,
        out_shape=out_shape,
        out_specs=out_specs,
        scratch_shapes=list(scratch),
        input_output_aliases=aliases or {},
        compiler_params=pltpu.CompilerParams(vmem_limit_bytes=VMEM_LIMIT),
        cost_estimate=pl.CostEstimate(
            flops=flops, bytes_accessed=rows * 1024 * 12, transcendentals=rows * keys * HEADS
        ),
    )


def carried(rows):
    return [
        jax.ShapeDtypeStruct((rows, HEADS * HEAD), jnp.float32),
        jax.ShapeDtypeStruct((rows, HEAD), jnp.float32),
    ]


def near(flags, q, k, v, cores, halo, doc_queries, doc_keys, heads=4):
    tokens, blocks = q.shape[0], doc_keys.shape[0]
    return call(
        near_kernel, "near", heads,
        [scalars(), column(tokens, heads), column(tokens, heads), column(tokens, heads)]
        + both(tokens, heads) + both(BLOCK, heads) + [fixed((tokens, HEAD)), fixed((blocks, HEAD))],
        carried(tokens), [column(tokens, heads), fixed((tokens, HEAD))], tokens, 6 * BLOCK,
    )(flags, q, k, v, cores, cores, halo, halo, doc_queries, doc_keys)


def middle(flags, q, far, a1, a2, b1, d1, e1, o, lse, heads=2):
    tokens = q.shape[0]
    whole, half = column(tokens, heads), both(tokens // 2, heads)
    return call(
        middle_kernel, "middle", heads,
        [scalars(), whole] + both(tokens, heads) * len(far) + half * 5 + [whole, fixed((tokens, HEAD))],
        carried(tokens), [whole, fixed((tokens, HEAD))], tokens, 7 * BLOCK,
    )(flags, q, *[x for x in [*far, a1, a2, b1, d1, e1] for _ in (0, 1)], o, lse)


def answer(asked, chunk, j, heads=8):
    rows = chunk.shape[0]
    return call(
        answer_kernel, "answer", heads,
        [column(rows, heads, j * HEADS)] + both(rows, heads),
        jax.ShapeDtypeStruct((rows, HEADS * HEAD + HEAD), jnp.bfloat16),
        fixed((rows, HEADS * HEAD + HEAD)),
        rows, BLOCK, scratch=[pltpu.VMEM((rows, HEAD), jnp.float32)],
    )(asked, chunk, chunk)


def last(flags, late, r, o, lse, weight, gain, j, out, heads=8):
    rows, tokens = r.shape[0], o.shape[0]
    specs, args = [scalars()], [flags]
    if late:
        queries, b, c = late
        specs += [column(rows, heads, 0, j)] + both(rows, heads) * 2
        args += [queries, b, b, c, c]
    specs += [column(rows, heads), fixed((rows, HEAD), (0, HEADS)), column(rows, heads, 0, j)]
    specs += [fixed((rows, HEAD), (j, 0)), fixed(weight.shape), fixed(gain.shape)]
    args += [r, r, o, lse, weight, gain]
    if out is not None:
        specs.append(pl.BlockSpec(memory_space=pl.ANY))
        args.append(out)
    return call(
        last_kernel, "last", heads, specs,
        jax.ShapeDtypeStruct((tokens, HEADS * HEAD), jnp.bfloat16),
        fixed((rows, HEADS * HEAD), (j, 0)),
        rows, 2 * BLOCK, scratch=[pltpu.VMEM((rows, HEADS * HEAD), jnp.bfloat16)],
        aliases={len(args) - 1: 0} if out is not None else None,
        extra=2 * rows * weight.size,
    )(*args)


def doc_rows(docs):
    digits = jnp.concatenate([docs // 32, docs % 32]).astype(jnp.bfloat16)
    return jnp.zeros((16, 2 * HEADS * HEAD), jnp.bfloat16).at[0, : digits.size].set(digits)


def docs_of(row, tokens):
    digits = row[: 2 * tokens].astype(jnp.int32)
    return digits[:tokens] * 32 + digits[tokens:]


def body(queries, key_rows, value_rows, doc_ids, out_weight, out_gain):
    tokens = queries.shape[0]
    half = tokens // 2
    blocks = tokens // BLOCK
    lo = lax.axis_index("lo")
    z, core = lo // 2, lo % 2
    inner = ((z % 4) == 1) | ((z % 4) == 2)
    first_core = core == 0
    flags = jnp.stack([inner.astype(jnp.int32), core])

    x1 = jnp.concatenate([key_rows[:half], value_rows[:half]], axis=1)
    a1 = along_z(x1, NEIGHBOUR)
    q2 = jnp.concatenate([queries[:half], queries[half:]], axis=1)
    d1 = along_z(jnp.where(inner, x1, q2), ASK + TWO_HOPS)
    x2 = jnp.concatenate([key_rows[half:], value_rows[half:]], axis=1)
    x = jnp.concatenate([key_rows, value_rows], axis=1)
    y1 = across(x, "hi", 1)
    w1 = across(x, "hi", 4)
    docs = doc_ids + 1
    numbers = doc_rows(docs)
    cores = across(jnp.concatenate([x, numbers], axis=0), "lo", 1)

    a1, d1, x2, x, y1, w1 = together(a1, d1, x2, x, y1, w1)
    a2 = along_z(x2, NEIGHBOUR)
    e1 = along_z(jnp.where(inner, x2, d1), FORWARD + TWO_HOPS)
    b1 = along_z(a1, PASS_ON)
    y2 = across(x, "hi", 2)
    w2 = across(x, "hi", 8)
    answers = answer(d1, a1, 0)
    ends = jnp.where(first_core, x[:BLOCK], x[tokens - BLOCK :])
    ends = jnp.concatenate([ends, numbers], axis=0)

    e1, ends, answers = together(e1, ends, answers)
    a2, e1, b1 = together(a2, e1, b1)
    r1 = along_z(answers, ANSWER)
    c2 = along_z(e1, FORWARD)
    b2 = along_z(a2, PASS_ON)
    r2 = along_z(answer(d1, a2, 1), ANSWER)
    size = lax.axis_size("hi") * lax.axis_size("lo")
    edge = [(d, d + 1) for d in range(1, size - 1, 2)] + [(d, d - 1) for d in range(2, size, 2)]
    halo = lax.ppermute(ends, ("hi", "lo"), edge)

    core_docs = docs_of(cores[tokens], tokens)
    halo_docs = docs_of(halo[BLOCK], tokens)
    own = docs.reshape(blocks, BLOCK)
    before = jnp.where(first_core, halo_docs, core_docs)[tokens - BLOCK :]
    after = jnp.where(first_core, core_docs, halo_docs)[:BLOCK]
    padded = jnp.concatenate([before[None], own, after[None]], axis=0)
    side = [i if i % 2 == 0 else i + 2 for i in range(blocks)]
    beside = jnp.concatenate([padded[i : i + 1] for i in side], axis=0)
    doc_keys = jnp.concatenate([beside, own], axis=1)
    doc_queries = jnp.broadcast_to(docs[:, None], (tokens, HEAD))
    halo, r1 = together(halo, r1)
    o, lse = near(flags, queries, key_rows, value_rows, cores, halo, doc_queries, doc_keys)
    o, lse = middle(flags, queries, [y1, y2, w1, w2], a1, a2, b1, d1, e1, o, lse)
    gain = out_gain[None]
    out = last(flags, None, r1, o, lse, out_weight, gain, 0, None)
    return last(flags, (queries, b2, c2), r2, o, lse, out_weight, gain, 1, out)


def solution(mesh):
    rows = P(("hi", "lo"), None)
    return jax.shard_map(
        body,
        mesh=mesh,
        in_specs=(rows, rows, rows, P(("hi", "lo")), P(), P()),
        out_specs=rows,
        check_vma=False,
    )
```

```python
import functools
import math

import jax
import jax.numpy as jnp
import numpy as np
from jax import lax
from jax.experimental import pallas as pl
from jax.experimental.pallas import tpu as pltpu
from jax.sharding import PartitionSpec as P

HEADS = 8
HEAD = 128
BLOCK = 64
LOW = -1e30
VMEM_LIMIT = 32 * 1024 * 1024
SCALE = HEAD**-0.5 * math.log2(math.e)

NEIGHBOUR = [(z, z ^ 1) for z in range(8)]
PASS_ON = [(1, 2), (2, 1), (5, 6), (6, 5)]
TWO_HOPS = [(2, 0), (1, 3), (6, 4), (5, 7)]
FORWARD = [(3, 5), (7, 1), (0, 6), (4, 2)]
ASK = [(4, 1), (0, 5), (7, 2), (3, 6)]
ANSWER = [(b, a) for a, b in ASK]


def along_z(x, pairs):
    return lax.ppermute(x, "lo", [(2 * a + c, 2 * b + c) for a, b in pairs for c in (0, 1)])


def across(x, axis, mask):
    return lax.ppermute(x, axis, [(i, i ^ mask) for i in range(lax.axis_size(axis))])


def together(*values):
    return lax.optimization_barrier(values)


def scores(q, k):
    s = lax.dot_general(q, k, (((1,), (1,)), ((), ())), preferred_element_type=jnp.float32)
    return s * SCALE


def cat(parts):
    return jnp.concatenate(parts, axis=0)


def blockwise(q, k):
    return cat([scores(q[i * BLOCK : (i + 1) * BLOCK], keys) for i, keys in enumerate(k)])


def weighted(p, v):
    p = p.astype(jnp.bfloat16)
    return cat(
        [
            jnp.dot(p[i * BLOCK : (i + 1) * BLOCK], values, preferred_element_type=jnp.float32)
            for i, values in enumerate(v)
        ]
    )


def rows_of(x, i):
    return x[i * BLOCK : (i + 1) * BLOCK]


def per_block(arrays, n):
    return [cat([rows_of(x, i) for x in arrays]) for i in range(n)]


def soft(s, v):
    peak = jnp.max(s, axis=-1, keepdims=True)
    p = jnp.exp2(s - peak)
    total = jnp.sum(p, axis=-1, keepdims=True)
    return weighted(p, v), peak, total


def put_lanes(ref, first, columns, old=None):
    old = jnp.where(first == 0, 0.0, ref[...]) if old is None else old
    lane = lax.broadcasted_iota(jnp.int32, old.shape, 1)
    for g, value in enumerate(columns):
        old = jnp.where(lane == first + g, value, old)
    ref[...] = old


def get_lane(x, h):
    lane = lax.broadcasted_iota(jnp.int32, x.shape, 1)
    return jnp.sum(jnp.where(lane == h, x, 0.0), axis=-1, keepdims=True)


def heads_of(ref):
    return [slice(g * HEAD, (g + 1) * HEAD) for g in range(ref.shape[1] // HEAD)]


def near_kernel(flags, q, k, v, ck, cv, hk, hv, docq, dock, o, lse):
    n = q.shape[0] // BLOCK
    first_core = flags[1] == 0
    a = lax.broadcasted_iota(jnp.int32, (BLOCK, 2 * BLOCK), 0)
    b = lax.broadcasted_iota(jnp.int32, (BLOCK, 2 * BLOCK), 1)
    masks = [(b >= BLOCK) | (b >= a), (b >= BLOCK) | (b <= a)]
    seen = cat([(rows_of(docq[...], i) == dock[i : i + 1, :]) & masks[i % 2] for i in range(n)])

    def gather(x, edge, core):
        first = jnp.where(first_core, edge, rows_of(core, n - 1))
        final = jnp.where(first_core, rows_of(core, 0), edge)
        side = [first] + [rows_of(x, i - 1 if i % 2 == 0 else i + 1) for i in range(1, n - 1)] + [final]
        return [
            cat([side[i]] + [rows_of(x, j) for j in (i, i ^ 1, i ^ 2, i ^ 4)] + [rows_of(core, i)])
            for i in range(n)
        ]

    levels = []
    for at in heads_of(q):
        s = blockwise(q[:, at], gather(k[:, at], hk[:, at], ck[:, at]))
        s = jnp.concatenate([jnp.where(seen, s[:, : 2 * BLOCK], LOW), s[:, 2 * BLOCK :]], axis=1)
        acc, peak, total = soft(s, gather(v[:, at], hv[:, at], cv[:, at]))
        o[:, at] = acc * (1.0 / total)
        levels.append(peak + jnp.log2(total))
    put_lanes(lse, pl.program_id(0) * len(levels), levels)


def merge(s, values, others):
    acc, peak, total = soft(s, values)
    top = peak
    for _, level in others:
        top = jnp.maximum(top, level)
    w = jnp.exp2(peak - top)
    denom = w * total
    weights = [w]
    for _, level in others:
        weights.append(jnp.exp2(level - top))
        denom = denom + weights[-1]
    share = 1.0 / denom
    numer = (w * share) * acc
    for (out, _), w in zip(others, weights[1:]):
        numer = numer + (w * share) * out
    return numer, top, denom


def middle_kernel(flags, q, *refs):
    far, rest = refs[:8], refs[8:]
    (a1k, a1v, a2k, a2v, b1k, b1v, d1k, d1v, e1k, e1v, o_in, lse_in, o, lse) = rest
    inner = flags[0] == 1
    half = q.shape[0] // 2
    n = half // BLOCK
    outs = [[], []]
    first = pl.program_id(0) * len(heads_of(q))
    for j in range(2):
        rows = slice(j * half, (j + 1) * half)
        old = lse_in[rows, :]
        for g, at in enumerate(heads_of(q)):

            def sets(far, a1, a2, b1, d1, e1):
                arrays = [x[rows, at] for x in far]
                if j == 0:
                    arrays += [a1[:, at], jnp.where(inner, b1[:, at], d1[:, at]), e1[:, at], e1[:, at]]
                else:
                    arrays += [a2[:, at], e1[:, at]]
                return per_block(arrays, n)

            s = blockwise(q[rows, at], sets(far[0::2], a1k, a2k, b1k, d1k, e1k))
            tail = s[:, 6 * BLOCK :] if j == 0 else s[:, 4 * BLOCK :]
            lane = lax.broadcasted_iota(jnp.int32, tail.shape, 1)
            seen = (inner & (lane < BLOCK)) if j == 0 else ((lane < BLOCK) | jnp.logical_not(inner))
            s = jnp.concatenate([s[:, : s.shape[1] - 2 * BLOCK], jnp.where(seen, tail, LOW)], axis=1)
            values = sets(far[1::2], a1v, a2v, b1v, d1v, e1v)
            out, top, denom = merge(s, values, [(o_in[rows, at], get_lane(old, first + g))])
            o[rows, at] = out
            outs[j].append(top + jnp.log2(denom))
    put_lanes(lse, first, [cat(pair) for pair in zip(*outs)])


def answer_kernel(q, k, v, packed, lse):
    n = q.shape[0] // BLOCK
    heads = heads_of(q)
    first = pl.program_id(0) * len(heads)
    old = jnp.where(first == 0, 0.0, lse[...])
    lane = lax.broadcasted_iota(jnp.int32, old.shape, 1)
    for g, at in enumerate(heads):
        acc, peak, total = soft(blockwise(q[:, at], per_block([k[:, at]], n)), per_block([v[:, at]], n))
        start = pl.multiple_of((first + g) * HEAD, HEAD)
        packed[:, pl.ds(start, HEAD)] = (acc * (1.0 / total)).astype(jnp.bfloat16)
        level = peak + jnp.log2(total)
        for part_at in range(3):
            part = level.astype(jnp.bfloat16).astype(jnp.float32)
            old = jnp.where(lane == first + g + HEADS * part_at, part, old)
            level = level - part
    lse[...] = old

    @pl.when(pl.program_id(0) == pl.num_programs(0) - 1)
    def _():
        packed[:, HEADS * HEAD :] = lse[...].astype(jnp.bfloat16)


def finish(att, w, gain, out):
    projected = jnp.dot(att[...], w[...], preferred_element_type=jnp.float32)
    mean = jnp.mean(projected * projected, axis=-1, keepdims=True)
    out[...] = (projected * lax.rsqrt(mean + 1e-06) * gain[...]).astype(jnp.bfloat16)


def last_kernel(flags, *refs):
    late = None
    if len(refs) > 8:
        late, refs = refs[:5], refs[5:]
    r_o, r_lse, o_in, lse_in, w, gain = refs[:6]
    out, att = refs[-2:]
    heads = heads_of(o_in)
    first = pl.program_id(0) * len(heads)
    inner = flags[0] == 1
    x = r_lse[...].astype(jnp.float32)
    lane = lax.broadcasted_iota(jnp.int32, x.shape, 1)
    old = lse_in[...]
    for g, at in enumerate(heads):
        mine = ((lane & (HEADS - 1)) == first + g) & (lane < 3 * HEADS)
        level = jnp.sum(jnp.where(mine, x, 0.0), axis=-1, keepdims=True)
        level = jnp.where(inner, LOW, level)
        answered = (r_o[:, at].astype(jnp.float32), level)
        held = (o_in[:, at], get_lane(old, first + g))
        if late is None:
            top = jnp.maximum(level, held[1])
            ways = [jnp.exp2(l - top) for _, l in (held, answered)]
            share = 1.0 / (ways[0] + ways[1])
            merged = (ways[0] * share) * held[0] + (ways[1] * share) * answered[0]
        else:
            q, bk, bv, ck, cv = late
            n = q.shape[0] // BLOCK
            s = blockwise(q[:, at], per_block([bk[:, at], ck[:, at]], n))
            s = jnp.where(inner, s, LOW)
            merged, _, _ = merge(s, per_block([bv[:, at], cv[:, at]], n), [held, answered])
        att[:, pl.ds(pl.multiple_of((first + g) * HEAD, HEAD), HEAD)] = merged.astype(jnp.bfloat16)

    @pl.when(pl.program_id(0) == pl.num_programs(0) - 1)
    def _():
        finish(att, w, gain, out)


def column(rows, heads, first=0, row=0):
    return pl.BlockSpec((rows, heads * HEAD), lambda h: (row, first // heads + h))


def both(rows, heads, row=0):
    return [column(rows, heads, 0, row), column(rows, heads, HEADS, row)]


def fixed(shape, index=(0, 0)):
    return pl.BlockSpec(shape, lambda h: index)


def scalars():
    return pl.BlockSpec(memory_space=pltpu.SMEM)


def call(kernel, name, heads, in_specs, out_shape, out_specs, rows, keys, scratch=(), aliases=None, extra=0):
    flops = 4 * rows * keys * HEAD * HEADS + extra
    return pl.pallas_call(
        kernel,
        name=name,
        grid=(HEADS // heads,),
        in_specs=in_specs,
        out_shape=out_shape,
        out_specs=out_specs,
        scratch_shapes=list(scratch),
        input_output_aliases=aliases or {},
        compiler_params=pltpu.CompilerParams(vmem_limit_bytes=VMEM_LIMIT),
        cost_estimate=pl.CostEstimate(
            flops=flops, bytes_accessed=rows * 1024 * 12, transcendentals=rows * keys * HEADS
        ),
    )


def carried(rows):
    return [
        jax.ShapeDtypeStruct((rows, HEADS * HEAD), jnp.float32),
        jax.ShapeDtypeStruct((rows, HEAD), jnp.float32),
    ]


def near(flags, q, k, v, cores, halo, doc_queries, doc_keys, heads=4):
    tokens, blocks = q.shape[0], doc_keys.shape[0]
    return call(
        near_kernel, "near", heads,
        [scalars(), column(tokens, heads), column(tokens, heads), column(tokens, heads)]
        + both(tokens, heads) + both(BLOCK, heads) + [fixed((tokens, HEAD)), fixed((blocks, HEAD))],
        carried(tokens), [column(tokens, heads), fixed((tokens, HEAD))], tokens, 6 * BLOCK,
    )(flags, q, k, v, cores, cores, halo, halo, doc_queries, doc_keys)


def middle(flags, q, far, a1, a2, b1, d1, e1, o, lse, heads=2):
    tokens = q.shape[0]
    whole, half = column(tokens, heads), both(tokens // 2, heads)
    return call(
        middle_kernel, "middle", heads,
        [scalars(), whole] + both(tokens, heads) * len(far) + half * 5 + [whole, fixed((tokens, HEAD))],
        carried(tokens), [whole, fixed((tokens, HEAD))], tokens, 7 * BLOCK,
    )(flags, q, *[x for x in [*far, a1, a2, b1, d1, e1] for _ in (0, 1)], o, lse)


def answer(asked, chunk, j, heads=8):
    rows = chunk.shape[0]
    return call(
        answer_kernel, "answer", heads,
        [column(rows, heads, j * HEADS)] + both(rows, heads),
        jax.ShapeDtypeStruct((rows, HEADS * HEAD + HEAD), jnp.bfloat16),
        fixed((rows, HEADS * HEAD + HEAD)),
        rows, BLOCK, scratch=[pltpu.VMEM((rows, HEAD), jnp.float32)],
    )(asked, chunk, chunk)


def last(flags, late, r, o, lse, weight, gain, j, out, heads=8):
    rows, tokens = r.shape[0], o.shape[0]
    specs, args = [scalars()], [flags]
    if late:
        queries, b, c = late
        specs += [column(rows, heads, 0, j)] + both(rows, heads) * 2
        args += [queries, b, b, c, c]
    specs += [column(rows, heads), fixed((rows, HEAD), (0, HEADS)), column(rows, heads, 0, j)]
    specs += [fixed((rows, HEAD), (j, 0)), fixed(weight.shape), fixed(gain.shape)]
    args += [r, r, o, lse, weight, gain]
    if out is not None:
        specs.append(pl.BlockSpec(memory_space=pl.ANY))
        args.append(out)
    return call(
        last_kernel, "last", heads, specs,
        jax.ShapeDtypeStruct((tokens, HEADS * HEAD), jnp.bfloat16),
        fixed((rows, HEADS * HEAD), (j, 0)),
        rows, 2 * BLOCK, scratch=[pltpu.VMEM((rows, HEADS * HEAD), jnp.bfloat16)],
        aliases={len(args) - 1: 0} if out is not None else None,
        extra=2 * rows * weight.size,
    )(*args)


def doc_rows(docs):
    digits = jnp.concatenate([docs // 32, docs % 32]).astype(jnp.bfloat16)
    return jnp.zeros((16, 2 * HEADS * HEAD), jnp.bfloat16).at[0, : digits.size].set(digits)


def docs_of(row, tokens):
    digits = row[: 2 * tokens].astype(jnp.int32)
    return digits[:tokens] * 32 + digits[tokens:]


def body(queries, key_rows, value_rows, doc_ids, out_weight, out_gain):
    tokens = queries.shape[0]
    half = tokens // 2
    blocks = tokens // BLOCK
    lo = lax.axis_index("lo")
    z, core = lo // 2, lo % 2
    inner = ((z % 4) == 1) | ((z % 4) == 2)
    first_core = core == 0
    flags = jnp.stack([inner.astype(jnp.int32), core])

    x1 = jnp.concatenate([key_rows[:half], value_rows[:half]], axis=1)
    a1 = along_z(x1, NEIGHBOUR)
    q2 = jnp.concatenate([queries[:half], queries[half:]], axis=1)
    d1 = along_z(jnp.where(inner, x1, q2), ASK + TWO_HOPS)
    x2 = jnp.concatenate([key_rows[half:], value_rows[half:]], axis=1)
    x = jnp.concatenate([key_rows, value_rows], axis=1)
    y1 = across(x, "hi", 1)
    w1 = across(x, "hi", 4)
    docs = doc_ids + 1
    numbers = doc_rows(docs)
    cores = across(jnp.concatenate([x, numbers], axis=0), "lo", 1)

    a1, d1, x2, x, y1, w1 = together(a1, d1, x2, x, y1, w1)
    a2 = along_z(x2, NEIGHBOUR)
    e1 = along_z(jnp.where(inner, x2, d1), FORWARD + TWO_HOPS)
    b1 = along_z(a1, PASS_ON)
    y2 = across(x, "hi", 2)
    w2 = across(x, "hi", 8)
    answers = answer(d1, a1, 0)
    ends = jnp.where(first_core, x[:BLOCK], x[tokens - BLOCK :])
    ends = jnp.concatenate([ends, numbers], axis=0)

    e1, ends, answers = together(e1, ends, answers)
    a2, e1, b1 = together(a2, e1, b1)
    r1 = along_z(answers, ANSWER)
    c2 = along_z(e1, FORWARD)
    b2 = along_z(a2, PASS_ON)
    r2 = along_z(answer(d1, a2, 1), ANSWER)
    size = lax.axis_size("hi") * lax.axis_size("lo")
    edge = [(d, d + 1) for d in range(1, size - 1, 2)] + [(d, d - 1) for d in range(2, size, 2)]
    halo = lax.ppermute(ends, ("hi", "lo"), edge)

    core_docs = docs_of(cores[tokens], tokens)
    halo_docs = docs_of(halo[BLOCK], tokens)
    own = docs.reshape(blocks, BLOCK)
    before = jnp.where(first_core, halo_docs, core_docs)[tokens - BLOCK :]
    after = jnp.where(first_core, core_docs, halo_docs)[:BLOCK]
    padded = jnp.concatenate([before[None], own, after[None]], axis=0)
    side = [i if i % 2 == 0 else i + 2 for i in range(blocks)]
    beside = jnp.concatenate([padded[i : i + 1] for i in side], axis=0)
    doc_keys = jnp.concatenate([beside, own], axis=1)
    doc_queries = jnp.broadcast_to(docs[:, None], (tokens, HEAD))
    halo, r1 = together(halo, r1)
    o, lse = near(flags, queries, key_rows, value_rows, cores, halo, doc_queries, doc_keys)
    o, lse = middle(flags, queries, [y1, y2, w1, w2], a1, a2, b1, d1, e1, o, lse)
    gain = out_gain[None]
    out = last(flags, None, r1, o, lse, out_weight, gain, 0, None)
    return last(flags, (queries, b2, c2), r2, o, lse, out_weight, gain, 1, out)


def solution(mesh):
    rows = P(("hi", "lo"), None)
    return jax.shard_map(
        body,
        mesh=mesh,
        in_specs=(rows, rows, rows, P(("hi", "lo")), P(), P()),
        out_specs=rows,
        check_vma=False,
    )
```
